32 devices in a mesh: recv: 8 (over y, x, core), seg: 4 (over z).
Axes of the slice: x: 2, y: 2, z: 4, core: 2. Of those that a mesh axis runs over, the one named last changes fastest.
Arguments:
- raw_data: float32 [8, 512, 2048], P('seg', 'recv'), may hold values from -210 to 210
- row_owner: int32 [512, 1], P('recv'), may hold values from 0 to 7; in each aligned block of 64 rows (0 to 63, 64 to 127, ...) at most 16 rows name the same one
- source_blocks: int32 [2], replicated, may hold values from 0 to 7, as said below
Outputs:
- correlations: bfloat16 [2, 128, 1024, 512], P(None, 'seg', 'recv')
The draws below stay inside these ranges and needn't reach their ends.
Inputs may be any that keep to these rules, and one draw needn't show every extreme that they name: `row_owner`: within the rows of one device (aligned blocks of 64 rows) no owner is named by more than 16 rows, a bound that some block reaches. `source_blocks`: the ids are distinct, and one of them is always the last block; block b covers channel slots b * 128 to (b + 1) * 128 - 1.
All inputs are finite; a program needn't handle non-finite values. Where the reference program divides by a largest or mean magnitude, that divisor is 1e-20 or more.
Results may differ from the reference program's by a relative error of at most 0.0068.
Values may be sent and summed in bfloat16 or wider, within the bound.
No kernel may reach another device: no remote copies, remote signals or barrier semaphores. Data moves between devices by JAX's collectives and lax.ppermute only.
A program may use at most 128 MiB of HBM per device.

```python
import math
import jax
import jax.numpy as jnp
import numpy as np
from jax import lax

WIN = 512
NB = 128
SRC_W = 128
SRC_BLK = 2
WINS = 4
RAW_DEV = 64
CAP = 16
RCV_SLOTS = 128
RAW_ROWS = 512
CHANNELS = 1024
SEGMENTS = 8
SAMP = 2048
N_RECV = 8


def draw_raw_data(key, part):
    key_base, key_scale = jax.random.split(key, 2)
    block_count = SAMP // NB
    base = jnp.clip(jax.random.normal(key_base, (SEGMENTS, RAW_ROWS, block_count, NB), jnp.float32), -5.0, 5.0)
    scales = jnp.exp(jax.random.uniform(key_scale, (SEGMENTS, RAW_ROWS, block_count, 1), jnp.float32, 0.0, math.log(10.0)))
    values = base * scales
    return values.reshape(SEGMENTS, RAW_ROWS, SAMP)


def draw_source_blocks(key, part):
    key_order, key_place = jax.random.split(jax.random.fold_in(key, 17), 2)
    block_total = CHANNELS // SRC_W
    ordering = jax.random.permutation(key_order, block_total - 1)[:SRC_BLK].astype(jnp.int32)
    position = jax.random.randint(key_place, (), 0, SRC_BLK).astype(jnp.int32)
    places = jnp.arange(SRC_BLK, dtype=jnp.int32)
    return jnp.where(places == position, jnp.int32(block_total - 1), ordering).astype(jnp.int32)


def deal_out(stream_key, own, number, rows, number_of, top, most, skew):
    sequence = jax.random.permutation(stream_key, number_of)
    heavy_load, usual = shares(number_of, rows * top, most, skew, True), shares(number_of, rows * top, most, skew, False)
    places = jnp.arange(number_of)

    def named(lengths, rotation):
        used = int((lengths > 0).sum())
        fixed = max(1, used // 4)
        shifted = fixed + (places - fixed + rotation * (used - fixed)) % max(1, number_of - fixed)
        return jnp.zeros((number_of,), jnp.int32).at[sequence[jnp.where(places < fixed, places, shifted)]].set(jnp.asarray(lengths, jnp.int32))

    lengths = jnp.where(number % 4 == 0, named(heavy_load, number // 4), named(usual, number - number // 4 - 1))
    mixed = jax.random.permutation(jax.random.fold_in(own, 3), number_of)
    donor, sink = mixed[0:number_of // 2 * 2:2], mixed[1:number_of // 2 * 2:2]
    margin = jnp.minimum(lengths[donor] - 1, most - lengths[sink]) // 2
    margin = jnp.where((donor == sequence[0]) | (sink == sequence[0]) | (lengths[sink] == 0), 0, jnp.maximum(margin, 0))
    shifted = jax.random.randint(jax.random.fold_in(own, 4), (number_of // 2,), 0, 1 << 20) % (margin + 1)
    lengths = lengths.at[donor].add(-shifted).at[sink].add(shifted)
    items = jnp.searchsorted(jnp.cumsum(lengths), jnp.arange(rows * top), side="right").astype(jnp.int32)
    grid = items.reshape(top, rows).T
    grid = grid[jax.random.permutation(jax.random.fold_in(own, 1), rows)]
    rotation = jax.random.randint(jax.random.fold_in(own, 2), (rows, 1), 0, top)
    return jnp.take_along_axis(grid, (jnp.arange(top)[None, :] + rotation) % top, axis=1)


def shares(amount, total, limit, slope, full):
    loads = [(1 << 20) // math.isqrt(standing ** slope) + 1 for standing in range(1, amount + 1)]
    largest = limit if full else min(limit, max(-(-total // amount), total * loads[0] // sum(loads)))
    least = 1 if total - largest >= amount - 1 else 0
    counts, rest = [largest] + [least] * (amount - 1), total - largest - least * (amount - 1)
    while rest > 0:
        movable = [i for i in range(1, amount) if counts[i] < largest] or [i for i in range(1, amount) if counts[i] < limit]
        mass, remaining = sum([loads[i] for i in movable]), rest
        for i in movable:
            extra = min(limit - counts[i], max(1, remaining * loads[i] // mass), rest)
            counts[i] = counts[i] + extra
            rest = rest - extra
    return np.array(counts)


def setup_inputs(seed: int = 0) -> dict:
    key_of = jax.random.split(jax.random.key(seed), 4)
    raw_data = draw_raw_data(jax.random.fold_in(key_of[3], 71), 0)
    row_owner_keys = jax.random.split(jax.random.fold_in(key_of[1], 1), RAW_ROWS // RAW_DEV)
    row_owner_turns = jax.random.permutation(jax.random.fold_in(key_of[1], 3), RAW_ROWS // RAW_DEV)
    row_owner = jax.vmap(lambda own, number: deal_out(jax.random.fold_in(key_of[1], 2), own, number, RAW_DEV, N_RECV, 1, CAP, 2))(row_owner_keys, row_owner_turns).reshape((RAW_ROWS, 1))
    source_blocks = draw_source_blocks(jax.random.fold_in(key_of[3], 71), 0)
    return {"raw_data": raw_data, "row_owner": row_owner, "source_blocks": source_blocks}


def forward_table(length):
    half_win = length // 2
    sample_ids = jnp.arange(length, dtype=jnp.int32)
    freq_ids = jnp.arange(half_win, dtype=jnp.int32)
    angles = (sample_ids[:, None] * freq_ids[None, :] % length).astype(jnp.float32) * (2.0 * math.pi / length)
    parity = jnp.where(sample_ids % 2 == 0, 1.0, -1.0).astype(jnp.float32)
    sines = jnp.where(freq_ids[None, :] == 0, parity[:, None], -jnp.sin(angles))
    return jnp.concatenate([jnp.cos(angles), sines], axis=1)

def inverse_table(length, window_total):
    half_win = length // 2
    lag_ids = jnp.arange(length, dtype=jnp.int32) - half_win
    freq_ids = jnp.arange(half_win, dtype=jnp.int32)
    angles = (freq_ids[:, None] * lag_ids[None, :] % length).astype(jnp.float32) * (2.0 * math.pi / length)
    factor = 1.0 / (length * math.sqrt(window_total * length))
    parity = jnp.where(lag_ids % 2 == 0, 1.0, -1.0).astype(jnp.float32)
    first = freq_ids[:, None] == 0
    cosine_rows = jnp.where(first, factor * jnp.ones_like(angles), 2.0 * factor * jnp.cos(angles))
    sine_rows = jnp.where(first, factor * parity[None, :] * jnp.ones_like(angles), -2.0 * factor * jnp.sin(angles))
    return jnp.concatenate([cosine_rows, sine_rows], axis=0).astype(jnp.bfloat16)

def normalize(series):
    blocks = series.reshape(series.shape[:-1] + (series.shape[-1] // NB, NB))
    amplitude = lax.optimization_barrier(jnp.mean(jnp.abs(blocks), axis=-1, keepdims=True)) + 1e-06
    return (blocks / amplitude).reshape(series.shape)

def spectra_of(series, dft_table):
    row_count = series.shape[0]
    windows = normalize(series).reshape(row_count, -1, dft_table.shape[0])
    return jnp.einsum('nkt,tj->nkj', windows, dft_table, precision=lax.Precision.HIGHEST).astype(jnp.bfloat16)

def cross_terms(source, receiver):
    half_win = source.shape[-1] // 2
    swapped = jnp.concatenate([receiver[..., half_win:], receiver[..., :half_win]], axis=-1)
    direct = jnp.einsum('skf,rkf->srf', source, receiver, precision=lax.Precision.HIGHEST)
    crossed = jnp.einsum('skf,rkf->srf', source, swapped, precision=lax.Precision.HIGHEST)
    interior = (jnp.arange(half_win) > 0).astype(direct.dtype)
    real_part = direct[..., :half_win] + interior * direct[..., half_win:]
    imag_part = interior * (crossed[..., :half_win] - crossed[..., half_win:]) + (1.0 - interior) * direct[..., half_win:]
    return jnp.concatenate([real_part, imag_part], axis=-1)

def reference(raw_data, row_owner, source_blocks):
    forward = forward_table(WIN)
    rows_first = jnp.transpose(raw_data, (1, 0, 2))
    row_spectra = spectra_of(rows_first, forward)
    owners = row_owner[:, 0].reshape(N_RECV, RAW_DEV)
    onehot = (owners[:, :, None] == jnp.arange(N_RECV, dtype=jnp.int32)[None, None, :]).astype(jnp.int32)
    rank_in_owner = lax.optimization_barrier(jnp.sum(onehot * (jnp.cumsum(onehot, axis=1) - 1), axis=2))
    senders = jnp.arange(N_RECV, dtype=jnp.int32)[:, None]
    slot_index = (owners * RCV_SLOTS + senders * CAP + rank_in_owner).reshape(-1).astype(jnp.int32)
    channel_spectra = jnp.zeros((CHANNELS, SEGMENTS * WINS, WIN), jnp.bfloat16).at[slot_index].set(row_spectra)
    source_rows = (source_blocks[:, None] * SRC_W + jnp.arange(SRC_W, dtype=jnp.int32)[None, :]).reshape(-1)
    sources = channel_spectra[source_rows].astype(jnp.float32)
    inverse = inverse_table(WIN, SEGMENTS * WINS).astype(jnp.float32)

    def owner_block(owner_id):
        receivers = lax.dynamic_slice_in_dim(channel_spectra, (owner_id * RCV_SLOTS).astype(jnp.int32), RCV_SLOTS, 0).astype(jnp.float32)
        stacked = lax.optimization_barrier(cross_terms(sources, receivers).astype(jnp.bfloat16)).astype(jnp.float32)
        lagged = jnp.einsum('srf,fl->srl', stacked, inverse, precision=lax.Precision.HIGHEST)
        return lagged.astype(jnp.bfloat16)
    blocks = lax.map(owner_block, jnp.arange(N_RECV, dtype=jnp.int32))
    merged = jnp.transpose(blocks, (1, 0, 2, 3)).reshape(SRC_BLK, SRC_W, CHANNELS, WIN)
    return merged
```

```python
import functools
import math

import jax
import jax.numpy as jnp
import numpy as np
from jax import lax
from jax.experimental import pallas as pl
from jax.experimental.pallas import tpu as pltpu
from jax.sharding import PartitionSpec as P

WIN = 512
NB = 128
SRC_W = 128
F8 = 8
F32 = jnp.float32
BF16 = jnp.bfloat16


def vmem():
    return pl.BlockSpec(memory_space=pltpu.VMEM)


def smem():
    return pl.BlockSpec(memory_space=pltpu.SMEM)


def forward_table(length):
    half = length // 2
    t = np.arange(length)[:, None]
    f = np.arange(half)[None, :]
    angles = 2.0 * math.pi * ((t * f) % length) / length
    parity = np.where(t % 2 == 0, 1.0, -1.0)
    sines = np.where(f == 0, parity, -np.sin(angles))
    return np.concatenate([np.cos(angles), sines], axis=1).astype(np.float32)


def inverse_table(length, window_total):
    half = length // 2
    lag = np.arange(length)[None, :] - half
    f = np.arange(half)[:, None]
    angles = 2.0 * math.pi * ((f * lag) % length) / length
    factor = 1.0 / (length * math.sqrt(window_total * length))
    parity = np.where(lag % 2 == 0, 1.0, -1.0)
    cosine = np.where(f == 0, factor, 2.0 * factor * np.cos(angles))
    sine = np.where(f == 0, factor * parity, -2.0 * factor * np.sin(angles))
    return np.concatenate([cosine, sine], axis=0).astype(np.float32)


def one_hots(own_col, own_row, key, blocks, slots, cap):
    rows = own_row.shape[1]
    earlier = lax.broadcasted_iota(jnp.int32, (rows, rows), 0) < lax.broadcasted_iota(
        jnp.int32, (rows, rows), 1
    )
    hits = jnp.where((own_col == own_row) & earlier, 1.0, 0.0)
    rank = jnp.sum(hits, axis=0, keepdims=True).astype(jnp.int32)
    slot = (own_row ^ key) * cap + rank
    pieces = [
        jnp.where(lax.broadcasted_iota(jnp.int32, (slots, rows), 0) == slot, 1.0, 0.0)
    ]
    for block in blocks:
        place = jnp.where(own_row == block, rank, -1)
        pieces.append(
            jnp.where(lax.broadcasted_iota(jnp.int32, (cap, rows), 0) == place, 1.0, 0.0)
        )
    return jnp.concatenate(pieces, axis=0).astype(BF16)


def place_rows(x_of, windows, select, slots, send_refs, src_ref, cap):
    for k in range(windows):
        y = jnp.dot(select, x_of(k), preferred_element_type=F32).astype(BF16)
        if len(send_refs) == 1:
            send_refs[0][k] = y[:slots]
        else:
            for d, ref in enumerate(send_refs):
                ref[k] = y[d * cap : (d + 1) * cap]
        src_ref[k] = y[slots:]


def first_kernel(slots, cap, raw, col, row, scal, t_hi, t_lo, x_ref, *outs):
    segs, rows, samples = raw.shape
    per = samples // WIN
    his, los = [], []
    for s in range(segs):
        for w in range(per):
            parts = []
            for b in range(WIN // NB):
                at = w * WIN + b * NB
                piece = raw[s, :, at : at + NB]
                amp = jnp.sum(jnp.abs(piece), axis=-1, keepdims=True) * (1.0 / NB) + 1e-06
                parts.append(piece / amp)
            x = jnp.concatenate(parts, axis=-1)
            hi = x.astype(BF16)
            his.append(hi)
            los.append((x - hi.astype(F32)).astype(BF16))
    hi = jnp.concatenate(his, axis=0)
    lo = jnp.concatenate(los, axis=0)
    dot = functools.partial(jnp.dot, preferred_element_type=F32)
    spec = dot(hi, t_lo[...]) + dot(lo, t_hi[...]) + dot(hi, t_hi[...])
    spec = spec.astype(BF16)
    windows = segs * per
    for k in range(windows):
        x_ref[k] = spec[k * rows : (k + 1) * rows]
    select = one_hots(col[...], row[...], scal[0], [scal[1], scal[2]], slots, cap)
    place_rows(
        lambda k: spec[k * rows : (k + 1) * rows], windows, select, slots, outs[:-1], outs[-1], cap
    )


def slot_kernel(slots, cap, x_ref, col, row, scal, *outs):
    select = one_hots(col[...], row[...], scal[0], [scal[1], scal[2]], slots, cap)
    place_rows(lambda k: x_ref[k], x_ref.shape[0], select, slots, outs[:-1], outs[-1], cap)


def turn_kernel(n_recv, *refs):
    recv, src = refs[:n_recv], refs[n_recv]
    bt, at = refs[n_recv + 1], refs[n_recv + 2]
    windows = src.shape[0]
    wide = 256
    eye = (
        lax.broadcasted_iota(jnp.int32, (wide, wide), 0)
        == lax.broadcasted_iota(jnp.int32, (wide, wide), 1)
    ).astype(BF16)
    turn = functools.partial(
        lax.dot_general, dimension_numbers=(((1,), (1,)), ((), ())), preferred_element_type=F32
    )
    for load, out in (
        (lambda k, ls: [r[k, :, ls] for r in recv], bt),
        (lambda k, ls: [src[k, :, ls]], at),
    ):
        n = out.shape[-1]
        for half in range(WIN // wide):
            ls = slice(half * wide, (half + 1) * wide)
            fs = slice(half * wide // F8, (half + 1) * wide // F8)
            for pair in range(windows // 2):
                both = jnp.concatenate(load(2 * pair, ls) + load(2 * pair + 1, ls), axis=0)
                y = turn(eye, both)
                y0 = y[:, :n].reshape(wide // F8, F8, n)
                y1 = y[:, n:].reshape(wide // F8, F8, n)
                out[fs, pair * 16 : (pair + 1) * 16, :] = jnp.concatenate(
                    [y0, y1], axis=1
                ).astype(BF16)


def cross_kernel(zbs, sblk, scal, *refs):
    n_in = 4 * zbs
    bre, bim = refs[:zbs], refs[zbs : 2 * zbs]
    are, aim = refs[2 * zbs : 3 * zbs], refs[3 * zbs : n_in]
    inv, out, stack = refs[n_in:]
    step = pl.program_id(0)
    nsrc, _, nrcv = stack.shape
    half_steps = WIN // 2 // (2 * F8)

    @pl.when(step < half_steps)
    def _():
        depth = zbs * bre[0].shape[1]
        eye = (
            lax.broadcasted_iota(jnp.int32, (nsrc, nsrc), 0)
            == lax.broadcasted_iota(jnp.int32, (nsrc, nsrc), 1)
        ).astype(BF16)
        lane_f = lax.broadcasted_iota(jnp.int32, (F8, depth), 1) % F8
        diag = lane_f == lax.broadcasted_iota(jnp.int32, (F8, depth), 0)
        turn = functools.partial(
            lax.dot_general, dimension_numbers=(((1,), (1,)), ((), ())), preferred_element_type=F32
        )
        dot = functools.partial(jnp.dot, preferred_element_type=F32)

        def spread(parts):
            v = jnp.concatenate(parts, axis=0)
            a = turn(eye, v)
            wide = jnp.where(diag[None], a[:, None, :], 0.0)
            return wide.reshape(nsrc * F8, depth).astype(BF16)

        reals, imags = [], []
        for j in range(2):
            wre = jnp.concatenate([r[j] for r in bre], axis=0)
            wim = jnp.concatenate([r[j] for r in bim], axis=0)
            lre = spread([r[j] for r in are])
            lim = spread([r[j] for r in aim])
            p1 = dot(lre, jnp.concatenate([wre, wim], axis=1)).reshape(nsrc, F8, 2 * nrcv)
            p2 = dot(lim, jnp.concatenate([wim, wre], axis=1)).reshape(nsrc, F8, 2 * nrcv)
            rr, ri = p1[..., :nrcv], p1[..., nrcv:]
            ii, ir = p2[..., :nrcv], p2[..., nrcv:]
            if j == 0:
                edge = (lax.broadcasted_iota(jnp.int32, (1, F8, nrcv), 1) == 0) & (step == 0)
                reals.append(rr + jnp.where(edge, 0.0, ii))
                imags.append(jnp.where(edge, ii, ri - ir))
            else:
                reals.append(rr + ii)
                imags.append(ri - ir)
        at = pl.multiple_of(step * 2 * F8, 2 * F8)
        stack[:, pl.ds(at, 2 * F8), :] = jnp.concatenate(reals, axis=1).astype(BF16)
        stack[:, pl.ds(WIN // 2 + at, 2 * F8), :] = jnp.concatenate(imags, axis=1).astype(BF16)

    @pl.when(step >= half_steps)
    def _():
        first = (step - half_steps) * sblk
        for s in range(sblk):
            slab = stack[first + s]
            res = lax.dot_general(
                slab, inv[...], (((0,), (0,)), ((), ())), preferred_element_type=F32
            ).astype(BF16)
            cap = out.shape[2]
            for d in range(out.shape[1]):
                out[s, d ^ scal[0] if out.shape[1] > 1 else d] = res[d * cap : (d + 1) * cap]


def local(raw_data, row_owner, source_blocks):
    recv_count = lax.axis_size("recv")
    seg_count = lax.axis_size("seg")
    segs, rows, samples = raw_data.shape
    windows = segs * samples // WIN
    cap = 2 * rows // recv_count
    slots = recv_count * cap
    blocks = source_blocks.shape[0]
    assert slots == SRC_W
    direct = cap % 16 == 0
    me = lax.axis_index("recv")
    seg = lax.axis_index("seg")
    key = me if direct else jnp.int32(0)
    scal = jnp.concatenate([jnp.reshape(key, (1,)).astype(jnp.int32), source_blocks])
    col = row_owner
    row = row_owner.reshape(1, rows)
    table = forward_table(WIN)
    t_hi = table.astype(BF16)
    t_lo = (table - t_hi.astype(np.float32)).astype(BF16)
    t_hi, t_lo = jnp.asarray(t_hi), jnp.asarray(t_lo)

    if direct:
        send_shapes = [jax.ShapeDtypeStruct((windows, cap, WIN), BF16)] * recv_count
    else:
        send_shapes = [jax.ShapeDtypeStruct((windows, slots, WIN), BF16)]
    src_shape = jax.ShapeDtypeStruct((windows, blocks * cap, WIN), BF16)
    x_shape = jax.ShapeDtypeStruct((windows, rows, WIN), BF16)

    first = pl.pallas_call(
        functools.partial(first_kernel, slots, cap),
        out_shape=[x_shape] + send_shapes + [src_shape],
        in_specs=[vmem(), vmem(), vmem(), smem(), vmem(), vmem()],
        out_specs=[vmem()] * (len(send_shapes) + 2),
        name="first",
    )(raw_data, col, row, scal, t_hi, t_lo)
    x, placed = first[0], [first[1:]]
    for d in range(1, seg_count):
        xd = lax.ppermute(x, "seg", [(i, i ^ d) for i in range(seg_count)])
        placed.append(
            pl.pallas_call(
                functools.partial(slot_kernel, slots, cap),
                out_shape=send_shapes + [src_shape],
                in_specs=[vmem(), vmem(), vmem(), smem()],
                out_specs=[vmem()] * (len(send_shapes) + 1),
                name="slots",
            )(xd, col, row, scal)
        )

    group = SRC_W // seg_count // cap
    low = group.bit_length() - 1
    high = recv_count.bit_length() - 1
    bts, ats = [], []
    for sent in placed:
        src = sent[-1]
        held = [[z * group + g for g in range(group)] for z in range(seg_count)]
        for bit in range(low, high):
            pairs = [
                (h * seg_count + z, (h ^ (1 << bit)) * seg_count + z)
                for z in range(seg_count)
                for h in held[z]
            ]
            got = lax.ppermute(src, ("recv", "seg"), pairs)
            has = (me >> bit) == ((seg * group) >> bit)
            src = jnp.where(has, src, got)
            held = [hs + [h ^ (1 << bit) for h in hs] for hs in held]
        src = src.reshape(windows, blocks, 1, cap, WIN)
        for bit in range(low):
            other = lax.ppermute(src, "recv", [(i, i ^ (1 << bit)) for i in range(recv_count)])
            upper = ((me >> bit) & 1) == 1
            src = jnp.concatenate(
                [jnp.where(upper, other, src), jnp.where(upper, src, other)], axis=2
            )
        src = src.reshape(windows, blocks * group * cap, WIN)
        if direct:
            recv = [sent[0]]
            for d in range(1, recv_count):
                recv.append(
                    lax.ppermute(sent[d], "recv", [(i, i ^ d) for i in range(recv_count)])
                )
        else:
            whole = sent[0].reshape(windows, recv_count, cap, WIN)
            whole = lax.all_to_all(whole, "recv", split_axis=1, concat_axis=1, tiled=True)
            recv = [whole.reshape(windows, slots, WIN)]
        nsrc = src.shape[1]
        bt, at = pl.pallas_call(
            functools.partial(turn_kernel, len(recv)),
            out_shape=[
                jax.ShapeDtypeStruct((WIN // F8, windows * F8, slots), BF16),
                jax.ShapeDtypeStruct((WIN // F8, windows * F8, nsrc), BF16),
            ],
            in_specs=[vmem()] * (len(recv) + 1),
            out_specs=[vmem()] * 2,
            name="turn",
        )(*recv, src)
        bts.append(bt)
        ats.append(at)

    inverse = jnp.asarray(inverse_table(WIN, seg_count * windows).astype(BF16))
    zbs = seg_count
    half_steps = WIN // 2 // (2 * F8)
    sblk = 4
    nd = recv_count if direct else 1
    depth = windows * F8

    def block(offset, width):
        return pl.BlockSpec(
            (2, depth, width), lambda i: (jnp.minimum(i, half_steps - 1) + offset, 0, 0)
        )

    out = pl.pallas_call(
        functools.partial(cross_kernel, zbs, sblk),
        out_shape=jax.ShapeDtypeStruct((nsrc, nd, slots // nd, WIN), BF16),
        grid=(half_steps + nsrc // sblk,),
        in_specs=[smem()]
        + [block(0, slots)] * zbs
        + [block(half_steps, slots)] * zbs
        + [block(0, nsrc)] * zbs
        + [block(half_steps, nsrc)] * zbs
        + [vmem()],
        out_specs=pl.BlockSpec(
            (sblk, nd, slots // nd, WIN), lambda i: (jnp.maximum(i - half_steps, 0), 0, 0, 0)
        ),
        scratch_shapes=[pltpu.VMEM((nsrc, WIN, slots), BF16)],
        name="cross",
    )(scal, *bts, *bts, *ats, *ats, inverse)
    return out.reshape(blocks, nsrc // blocks, slots, WIN)


def solution(mesh):
    placed = (P("seg", "recv", None), P("recv", None), P())
    return jax.shard_map(
        local, mesh=mesh, in_specs=placed, out_specs=P(None, "seg", "recv", None), check_vma=False
    )
```

```python
import functools
import math

import jax
import jax.numpy as jnp
import numpy as np
from jax import lax
from jax.experimental import pallas as pl
from jax.experimental.pallas import tpu as pltpu
from jax.sharding import PartitionSpec as P


WIN = 512
NB = 128
SRC_W = 128
F8 = 8
F32 = jnp.float32
BF16 = jnp.bfloat16


def vmem():
    return pl.BlockSpec(memory_space=pltpu.VMEM)


def smem():
    return pl.BlockSpec(memory_space=pltpu.SMEM)


def forward_table(length):
    half = length // 2
    t = np.arange(length)[:, None]
    f = np.arange(half)[None, :]
    angles = 2.0 * math.pi * ((t * f) % length) / length
    parity = np.where(t % 2 == 0, 1.0, -1.0)
    sines = np.where(f == 0, parity, -np.sin(angles))
    return np.concatenate([np.cos(angles), sines], axis=1).astype(np.float32)


def inverse_table(length, window_total):
    half = length // 2
    lag = np.arange(length)[None, :] - half
    f = np.arange(half)[:, None]
    angles = 2.0 * math.pi * ((f * lag) % length) / length
    factor = 1.0 / (length * math.sqrt(window_total * length))
    parity = np.where(lag % 2 == 0, 1.0, -1.0)
    cosine = np.where(f == 0, factor, 2.0 * factor * np.cos(angles))
    sine = np.where(f == 0, factor * parity, -2.0 * factor * np.sin(angles))
    return np.concatenate([cosine, sine], axis=0).astype(np.float32)


def one_hots(own_row, blocks, slots, cap):
    rows = own_row.shape[1]
    own_col = jnp.broadcast_to(own_row, (rows, rows)).astype(F32).T.astype(jnp.int32)
    earlier = lax.broadcasted_iota(jnp.int32, (rows, rows), 0) < lax.broadcasted_iota(
        jnp.int32, (rows, rows), 1
    )
    hits = jnp.where((own_col == own_row) & earlier, 1.0, 0.0)
    rank = jnp.sum(hits, axis=0, keepdims=True).astype(jnp.int32)
    slot = own_row * cap + rank
    pieces = [
        jnp.where(lax.broadcasted_iota(jnp.int32, (slots, rows), 0) == slot, 1.0, 0.0)
    ]
    for block in blocks:
        place = jnp.where(own_row == block, rank, -1)
        pieces.append(
            jnp.where(lax.broadcasted_iota(jnp.int32, (cap, rows), 0) == place, 1.0, 0.0)
        )
    return jnp.concatenate(pieces, axis=0).astype(BF16)


def place_rows(x_of, windows, select, slots, send_ref, src_ref, cap):
    for k in range(windows):
        y = jnp.dot(select, x_of(k), preferred_element_type=F32).astype(BF16)
        if len(send_ref.shape) == 3:
            send_ref[k] = y[:slots]
        else:
            for d in range(slots // cap):
                send_ref[d, k] = y[d * cap : (d + 1) * cap]
        src_ref[k] = y[slots:]


def first_kernel(slots, cap, raw, row, blocks, t_hi, t_lo, x_ref, send_ref, src_ref):
    segs, rows, samples = raw.shape
    per = samples // WIN
    his, los = [], []
    for s in range(segs):
        for w in range(per):
            parts = []
            for b in range(WIN // NB):
                at = w * WIN + b * NB
                piece = raw[s, :, at : at + NB]
                amp = jnp.sum(jnp.abs(piece), axis=-1, keepdims=True) * (1.0 / NB) + 1e-06
                parts.append(piece / amp)
            x = jnp.concatenate(parts, axis=-1)
            hi = x.astype(BF16)
            his.append(hi)
            los.append((x - hi.astype(F32)).astype(BF16))
    hi = jnp.concatenate(his, axis=0)
    lo = jnp.concatenate(los, axis=0)
    dot = functools.partial(jnp.dot, preferred_element_type=F32)
    spec = dot(hi, t_lo[...]) + dot(lo, t_hi[...]) + dot(hi, t_hi[...])
    spec = spec.astype(BF16)
    windows = segs * per
    for k in range(windows):
        x_ref[k] = spec[k * rows : (k + 1) * rows]
    select = one_hots(row[...], [blocks[b] for b in range(blocks.shape[0])], slots, cap)
    place_rows(
        lambda k: spec[k * rows : (k + 1) * rows], windows, select, slots, send_ref, src_ref, cap
    )


def slot_kernel(slots, cap, x_ref, row, blocks, send_ref, src_ref):
    select = one_hots(row[...], [blocks[b] for b in range(blocks.shape[0])], slots, cap)
    place_rows(lambda k: x_ref[k], x_ref.shape[0], select, slots, send_ref, src_ref, cap)


def turn_kernel(upper, recv, src, other, bt, at):
    windows = src.shape[0]
    wide = 256
    eye = (
        lax.broadcasted_iota(jnp.int32, (wide, wide), 0)
        == lax.broadcasted_iota(jnp.int32, (wide, wide), 1)
    ).astype(BF16)
    turn = functools.partial(
        lax.dot_general, dimension_numbers=(((1,), (1,)), ((), ())), preferred_element_type=F32
    )

    def received(k, ls):
        if len(recv.shape) == 3:
            return [recv[k, :, ls]]
        return [recv[d, k, :, ls] for d in range(recv.shape[0])]

    def sources(k, ls):
        mine, theirs = src[k, :, ls], other[k, :, ls]
        swap = upper[0] == 1
        return [jnp.where(swap, theirs, mine), jnp.where(swap, mine, theirs)]

    for load, out in ((received, bt), (sources, at)):
        n = out.shape[-1]
        for half in range(WIN // wide):
            ls = slice(half * wide, (half + 1) * wide)
            fs = slice(half * wide // F8, (half + 1) * wide // F8)
            for pair in range(windows // 2):
                both = jnp.concatenate(load(2 * pair, ls) + load(2 * pair + 1, ls), axis=0)
                y = turn(eye, both)
                y0 = y[:, :n].reshape(wide // F8, F8, n)
                y1 = y[:, n:].reshape(wide // F8, F8, n)
                out[fs, pair * 16 : (pair + 1) * 16, :] = jnp.concatenate(
                    [y0, y1], axis=1
                ).astype(BF16)


def cross_kernel(zbs, sblk, *refs):
    n_in = 4 * zbs
    bre, bim = refs[:zbs], refs[zbs : 2 * zbs]
    are, aim = refs[2 * zbs : 3 * zbs], refs[3 * zbs : n_in]
    inv, out, stack = refs[n_in:]
    step = pl.program_id(0)
    nsrc, _, nrcv = stack.shape
    half_steps = WIN // 2 // (2 * F8)

    @pl.when(step < half_steps)
    def _():
        depth = zbs * bre[0].shape[1]
        eye = (
            lax.broadcasted_iota(jnp.int32, (nsrc, nsrc), 0)
            == lax.broadcasted_iota(jnp.int32, (nsrc, nsrc), 1)
        ).astype(BF16)
        lane_f = lax.broadcasted_iota(jnp.int32, (F8, depth), 1) % F8
        diag = lane_f == lax.broadcasted_iota(jnp.int32, (F8, depth), 0)
        turn = functools.partial(
            lax.dot_general, dimension_numbers=(((1,), (1,)), ((), ())), preferred_element_type=F32
        )
        dot = functools.partial(jnp.dot, preferred_element_type=F32)

        def spread(parts):
            v = jnp.concatenate(parts, axis=0)
            a = turn(eye, v)
            wide = jnp.where(diag[None], a[:, None, :], 0.0)
            return wide.reshape(nsrc * F8, depth).astype(BF16)

        reals, imags = [], []
        for j in range(2):
            wre = jnp.concatenate([r[j] for r in bre], axis=0)
            wim = jnp.concatenate([r[j] for r in bim], axis=0)
            lre = spread([r[j] for r in are])
            lim = spread([r[j] for r in aim])
            p1 = dot(lre, jnp.concatenate([wre, wim], axis=1)).reshape(nsrc, F8, 2 * nrcv)
            p2 = dot(lim, jnp.concatenate([wim, wre], axis=1)).reshape(nsrc, F8, 2 * nrcv)
            rr, ri = p1[..., :nrcv], p1[..., nrcv:]
            ii, ir = p2[..., :nrcv], p2[..., nrcv:]
            if j == 0:
                edge = (lax.broadcasted_iota(jnp.int32, (1, F8, nrcv), 1) == 0) & (step == 0)
                reals.append(rr + jnp.where(edge, 0.0, ii))
                imags.append(jnp.where(edge, ii, ri - ir))
            else:
                reals.append(rr + ii)
                imags.append(ri - ir)
        at = pl.multiple_of(step * 2 * F8, 2 * F8)
        stack[:, pl.ds(at, 2 * F8), :] = jnp.concatenate(reals, axis=1).astype(BF16)
        stack[:, pl.ds(WIN // 2 + at, 2 * F8), :] = jnp.concatenate(imags, axis=1).astype(BF16)

    @pl.when(step >= half_steps)
    def _():
        first = (step - half_steps) * sblk
        slab = jnp.concatenate([stack[first + s] for s in range(sblk)], axis=1)
        res = lax.dot_general(
            slab, inv[...], (((0,), (0,)), ((), ())), preferred_element_type=F32
        ).astype(BF16)
        for s in range(sblk):
            out[s] = res[s * nrcv : (s + 1) * nrcv]


def steps(raw_data, row_owner, source_blocks):
    recv_count = lax.axis_size("recv")
    seg_count = lax.axis_size("seg")
    segs, rows, samples = raw_data.shape
    windows = segs * samples // WIN
    cap = 2 * rows // recv_count
    slots = recv_count * cap
    blocks = source_blocks.shape[0]
    assert slots == SRC_W
    direct = cap % 16 == 0
    me = lax.axis_index("recv")
    seg = lax.axis_index("seg")
    row = row_owner.reshape(1, rows)
    table = forward_table(WIN)
    t_hi = table.astype(BF16)
    t_lo = (table - t_hi.astype(np.float32)).astype(BF16)
    t_hi, t_lo = jnp.asarray(t_hi), jnp.asarray(t_lo)

    send_shape = (recv_count, windows, cap, WIN) if direct else (windows, slots, WIN)
    send_shape = jax.ShapeDtypeStruct(send_shape, BF16)
    src_shape = jax.ShapeDtypeStruct((windows, blocks * cap, WIN), BF16)
    x_shape = jax.ShapeDtypeStruct((windows, rows, WIN), BF16)

    x, send, src = pl.pallas_call(
        functools.partial(first_kernel, slots, cap),
        out_shape=[x_shape, send_shape, src_shape],
        in_specs=[vmem(), vmem(), smem(), vmem(), vmem()],
        out_specs=[vmem()] * 3,
        name="first",
    )(raw_data, row, source_blocks, t_hi, t_lo)
    placed = [(send, src)]
    for d in range(1, seg_count):
        xd = lax.ppermute(x, "seg", [(i, i ^ d) for i in range(seg_count)])
        placed.append(
            pl.pallas_call(
                functools.partial(slot_kernel, slots, cap),
                out_shape=[send_shape, src_shape],
                in_specs=[vmem(), vmem(), smem()],
                out_specs=[vmem()] * 2,
                name="slots",
            )(xd, row, source_blocks)
        )

    group = SRC_W // seg_count // cap
    low = group.bit_length() - 1
    high = recv_count.bit_length() - 1
    bts, ats = [], []
    for send, src in placed:
        if direct:
            recv = lax.all_to_all(send, "recv", split_axis=0, concat_axis=0, tiled=True)
        else:
            recv = send.reshape(windows, recv_count, cap, WIN)
            recv = lax.all_to_all(recv, "recv", split_axis=1, concat_axis=1, tiled=True)
            recv = recv.reshape(windows, slots, WIN)
        held = [[z * group + g for g in range(group)] for z in range(seg_count)]
        for bit in range(high - 1, low - 1, -1):
            pairs = [
                (h * seg_count + z, (h ^ (1 << bit)) * seg_count + z)
                for z in range(seg_count)
                for h in held[z]
            ]
            got = lax.ppermute(src, ("recv", "seg"), pairs)
            apart = (me ^ (seg * group)) >> low
            has = (apart & ((1 << (bit - low + 1)) - 1)) == 0
            src = jnp.where(has, src, got)
            held = [hs + [h ^ (1 << bit) for h in hs] for hs in held]
        swap = [[(i, i ^ (1 << bit)) for i in range(recv_count)] for bit in range(low)]
        for bit in range(low - 1):
            other = lax.ppermute(src, "recv", swap[bit])
            upper = ((me >> bit) & 1) == 1
            src = jnp.concatenate(
                [jnp.where(upper, other, src), jnp.where(upper, src, other)], axis=1
            )
        other = lax.ppermute(src, "recv", swap[low - 1])
        upper = ((me >> (low - 1)) & 1).reshape(1).astype(jnp.int32)
        nsrc = 2 * src.shape[1]
        bt, at = pl.pallas_call(
            turn_kernel,
            out_shape=[
                jax.ShapeDtypeStruct((WIN // F8, windows * F8, slots), BF16),
                jax.ShapeDtypeStruct((WIN // F8, windows * F8, nsrc), BF16),
            ],
            in_specs=[smem()] + [vmem()] * 3,
            out_specs=[vmem()] * 2,
            name="turn",
        )(upper, recv, src, other)
        bts.append(bt)
        ats.append(at)

    inverse = jnp.asarray(inverse_table(WIN, seg_count * windows).astype(BF16))
    zbs = seg_count
    half_steps = WIN // 2 // (2 * F8)
    sblk = cap
    depth = windows * F8

    def block(offset, width):
        return pl.BlockSpec(
            (2, depth, width), lambda i: (jnp.minimum(i, half_steps - 1) + offset, 0, 0)
        )

    def place(i):
        at = jnp.maximum(i - half_steps, 0)
        return (at % blocks) * group + at // blocks, 0, 0

    out = pl.pallas_call(
        functools.partial(cross_kernel, zbs, sblk),
        out_shape=jax.ShapeDtypeStruct((nsrc, slots, WIN), BF16),
        grid=(half_steps + nsrc // sblk,),
        in_specs=[block(0, slots)] * zbs
        + [block(half_steps, slots)] * zbs
        + [block(0, nsrc)] * zbs
        + [block(half_steps, nsrc)] * zbs
        + [vmem()],
        out_specs=pl.BlockSpec((sblk, slots, WIN), place),
        scratch_shapes=[pltpu.VMEM((nsrc, WIN, slots), BF16)],
        name="cross",
    )(*bts, *bts, *ats, *ats, inverse)
    return out.reshape(blocks, nsrc // blocks, slots, WIN)


def solution(mesh):
    placed = (P("seg", "recv", None), P("recv", None), P())
    return jax.shard_map(
        steps, mesh=mesh, in_specs=placed, out_specs=P(None, "seg", "recv", None), check_vma=False
    )
```

```python
import functools
import math

import jax
import jax.numpy as jnp
import numpy as np
from jax import lax
from jax.experimental import pallas as pl
from jax.experimental.pallas import tpu as pltpu
from jax.sharding import PartitionSpec as P


WIN = 512
NB = 128
SRC_W = 128
F8 = 8
F4 = 4
F32 = jnp.float32
BF16 = jnp.bfloat16


def vmem():
    return pl.BlockSpec(memory_space=pltpu.VMEM)


def smem():
    return pl.BlockSpec(memory_space=pltpu.SMEM)


def forward_table(length):
    half = length // 2
    t = np.arange(length)[:, None]
    f = np.arange(half)[None, :]
    angles = 2.0 * math.pi * ((t * f) % length) / length
    parity = np.where(t % 2 == 0, 1.0, -1.0)
    sines = np.where(f == 0, parity, -np.sin(angles))
    return np.concatenate([np.cos(angles), sines], axis=1).astype(np.float32)


def inverse_table(length, window_total):
    half = length // 2
    lag = np.arange(length)[None, :] - half
    f = np.arange(half)[:, None]
    angles = 2.0 * math.pi * ((f * lag) % length) / length
    factor = 1.0 / (length * math.sqrt(window_total * length))
    parity = np.where(lag % 2 == 0, 1.0, -1.0)
    cosine = np.where(f == 0, factor, 2.0 * factor * np.cos(angles))
    sine = np.where(f == 0, factor * parity, -2.0 * factor * np.sin(angles))
    return np.concatenate([cosine, sine], axis=0).astype(np.float32)


def columns(length):
    return np.arange(length).reshape(2, -1, F4).transpose(1, 0, 2).reshape(-1)


def one_hots(own_row, blocks, slots, cap):
    rows = own_row.shape[1]
    own_col = jnp.broadcast_to(own_row, (rows, rows)).astype(F32).T.astype(jnp.int32)
    earlier = lax.broadcasted_iota(jnp.int32, (rows, rows), 0) < lax.broadcasted_iota(
        jnp.int32, (rows, rows), 1
    )
    hits = jnp.where((own_col == own_row) & earlier, 1.0, 0.0)
    rank = jnp.sum(hits, axis=0, keepdims=True).astype(jnp.int32)
    slot = own_row * cap + rank
    pieces = [
        jnp.where(lax.broadcasted_iota(jnp.int32, (slots, rows), 0) == slot, 1.0, 0.0)
    ]
    for block in blocks:
        place = jnp.where(own_row == block, rank, -1)
        pieces.append(
            jnp.where(lax.broadcasted_iota(jnp.int32, (cap, rows), 0) == place, 1.0, 0.0)
        )
    return jnp.concatenate(pieces, axis=0).astype(BF16)


def place_rows(x_of, windows, select, slots, send_ref, src_ref, cap):
    for k in range(windows):
        y = jnp.dot(select, x_of(k), preferred_element_type=F32).astype(BF16)
        if len(send_ref.shape) == 3:
            send_ref[k] = y[:slots]
        else:
            for d in range(slots // cap):
                send_ref[d, k] = y[d * cap : (d + 1) * cap]
        src_ref[k] = y[slots:]


def first_kernel(slots, cap, raw, row, blocks, t_hi, t_lo, x_ref, send_ref, src_ref, sel_ref):
    segs, rows, samples = raw.shape
    per = samples // WIN
    his, los = [], []
    for s in range(segs):
        for w in range(per):
            parts = []
            for b in range(WIN // NB):
                at = w * WIN + b * NB
                piece = raw[s, :, at : at + NB]
                amp = jnp.sum(jnp.abs(piece), axis=-1, keepdims=True) * (1.0 / NB) + 1e-06
                parts.append(piece / amp)
            x = jnp.concatenate(parts, axis=-1)
            hi = x.astype(BF16)
            his.append(hi)
            los.append((x - hi.astype(F32)).astype(BF16))
    hi = jnp.concatenate(his, axis=0)
    lo = jnp.concatenate(los, axis=0)
    dot = functools.partial(jnp.dot, preferred_element_type=F32)
    spec = dot(hi, t_lo[...]) + dot(lo, t_hi[...]) + dot(hi, t_hi[...])
    spec = spec.astype(BF16)
    windows = segs * per
    for k in range(windows):
        x_ref[k] = spec[k * rows : (k + 1) * rows]
    select = one_hots(row[...], [blocks[b] for b in range(blocks.shape[0])], slots, cap)
    sel_ref[...] = select
    place_rows(
        lambda k: spec[k * rows : (k + 1) * rows], windows, select, slots, send_ref, src_ref, cap
    )


def slot_kernel(slots, cap, sel_ref, x_ref, send_ref, src_ref):
    place_rows(lambda k: x_ref[k], x_ref.shape[0], sel_ref[...], slots, send_ref, src_ref, cap)


def turn_kernel(start, upper, recv, src, other, bt, at):
    windows = bt.shape[1] // F8
    wide = 256
    eye = (
        lax.broadcasted_iota(jnp.int32, (wide, wide), 0)
        == lax.broadcasted_iota(jnp.int32, (wide, wide), 1)
    ).astype(BF16)
    turn = functools.partial(
        lax.dot_general, dimension_numbers=(((1,), (1,)), ((), ())), preferred_element_type=F32
    )

    def received(k, ls):
        if len(recv.shape) == 3:
            return [recv[k, :, ls]]
        return [recv[d, k, :, ls] for d in range(recv.shape[0])]

    def sources(k, ls):
        mine, theirs = src[start + k, :, ls], other[start + k, :, ls]
        swap = upper[0] == 1
        return [jnp.where(swap, theirs, mine), jnp.where(swap, mine, theirs)]

    for load, out in ((received, bt), (sources, at)):
        n = out.shape[-1]
        for half in range(WIN // wide):
            ls = slice(half * wide, (half + 1) * wide)
            fs = slice(half * wide // F8, (half + 1) * wide // F8)
            for pair in range(windows // 2):
                both = jnp.concatenate(load(2 * pair, ls) + load(2 * pair + 1, ls), axis=0)
                y = turn(eye, both)
                y0 = y[:, :n].reshape(wide // F8, F8, n)
                y1 = y[:, n:].reshape(wide // F8, F8, n)
                out[fs, pair * 16 : (pair + 1) * 16, :] = jnp.concatenate(
                    [y0, y1], axis=1
                ).astype(BF16)


def cross_kernel(zbs, sblk, per, *refs):
    b_refs, a_refs = refs[:zbs], refs[zbs : 2 * zbs]
    inv, out, stack = refs[2 * zbs :]
    step = pl.program_id(0)
    nsrc, _, nrcv = stack.shape
    half_steps = WIN // F8 // per

    @pl.when(step < half_steps)
    def _():
        depth = zbs * b_refs[0].shape[1]
        groups = depth // F8
        iota = functools.partial(lax.broadcasted_iota, jnp.int32)
        rep = (iota((nsrc * F4, nsrc), 0) // F4 == iota((nsrc * F4, nsrc), 1)).astype(BF16)
        diag = iota((F8, depth), 1) % F4 == iota((F8, depth), 0) % F4
        place = iota((1, F8, nrcv), 1)
        low = place < F4
        turn = functools.partial(
            lax.dot_general, dimension_numbers=(((1,), (1,)), ((), ())), preferred_element_type=F32
        )
        evens, odds = [], []
        for j in range(per):
            w = jnp.concatenate([r[j] for r in b_refs], axis=0)
            v = jnp.concatenate([r[j] for r in a_refs], axis=0)
            wide = turn(rep, v).reshape(nsrc * F4 // F8, F8, depth)
            left = jnp.where(diag[None], wide, 0.0).reshape(nsrc * F4, depth).astype(BF16)
            w3 = w.astype(F32).reshape(groups, F8, nrcv)
            turned = pltpu.roll(w3, F4, 1)
            turned = jnp.where(low, turned, -turned)
            if j == 0:
                zero, nyquist = (step == 0) & (place == 0), (step == 0) & (place == F4)
                turned = jnp.where(zero, 0.0, jnp.where(nyquist, w3, turned))
                w = jnp.where(nyquist, 0.0, w3).reshape(depth, nrcv).astype(BF16)
            right = jnp.concatenate([w, turned.reshape(depth, nrcv).astype(BF16)], axis=1)
            res = jnp.dot(left, right, preferred_element_type=F32)
            real = res[:, :nrcv].reshape(nsrc // 2, F8, nrcv)
            imag = res[:, nrcv:].reshape(nsrc // 2, F8, nrcv)
            evens.append(jnp.where(low, real, pltpu.roll(imag, F4, 1)))
            odds.append(jnp.where(low, pltpu.roll(real, F4, 1), imag))
        for j in range(0, per, 2):
            at = pl.multiple_of((step * per + j) * F8, 2 * F8)
            even, odd = (jnp.concatenate(h[j : j + 2], axis=1).astype(BF16) for h in (evens, odds))
            stack[: nsrc // 2, pl.ds(at, 2 * F8), :] = even
            stack[nsrc // 2 :, pl.ds(at, 2 * F8), :] = odd

    @pl.when(step >= half_steps)
    def _():
        each = sblk // 2
        first = (step - half_steps) * each
        slab = jnp.concatenate(
            [stack[p * (nsrc // 2) + first + s] for s in range(each) for p in range(2)], axis=1
        )
        res = lax.dot_general(
            slab, inv[...], (((0,), (0,)), ((), ())), preferred_element_type=F32
        ).astype(BF16)
        for s in range(sblk):
            out[s] = res[s * nrcv : (s + 1) * nrcv]


def double(src, seg_count, group, low, high):
    me, seg = lax.axis_index("recv"), lax.axis_index("seg")
    held = [[z * group + g for g in range(group)] for z in range(seg_count)]
    for bit in range(high - 1, low - 1, -1):
        pairs = [
            (h * seg_count + z, (h ^ (1 << bit)) * seg_count + z)
            for z in range(seg_count)
            for h in held[z]
        ]
        got = lax.ppermute(src, ("recv", "seg"), pairs)
        apart = (me ^ (seg * group)) >> low
        src = jnp.where((apart & ((1 << (bit - low + 1)) - 1)) == 0, src, got)
        held = [hs + [h ^ (1 << bit) for h in hs] for hs in held]
    return src


def steps(raw_data, row_owner, source_blocks):
    recv_count = lax.axis_size("recv")
    seg_count = lax.axis_size("seg")
    segs, rows, samples = raw_data.shape
    windows = segs * samples // WIN
    cap = 2 * rows // recv_count
    slots = recv_count * cap
    blocks = source_blocks.shape[0]
    assert slots == SRC_W
    direct = cap % 16 == 0
    me = lax.axis_index("recv")
    assert seg_count == 4
    row = row_owner.reshape(1, rows)
    table = forward_table(WIN)[:, columns(WIN)]
    t_hi = table.astype(BF16)
    t_lo = (table - t_hi.astype(np.float32)).astype(BF16)
    t_hi, t_lo = jnp.asarray(t_hi), jnp.asarray(t_lo)

    send_shape = (recv_count, windows, cap, WIN) if direct else (windows, slots, WIN)
    send_shape = jax.ShapeDtypeStruct(send_shape, BF16)
    src_shape = jax.ShapeDtypeStruct((windows, blocks * cap, WIN), BF16)
    x_shape = jax.ShapeDtypeStruct((windows, rows, WIN), BF16)

    picks = slots + blocks * cap
    x, send, src, select = pl.pallas_call(
        functools.partial(first_kernel, slots, cap),
        out_shape=[x_shape, send_shape, src_shape, jax.ShapeDtypeStruct((picks, rows), BF16)],
        in_specs=[vmem(), vmem(), smem(), vmem(), vmem()],
        out_specs=[vmem()] * 4,
        name="first",
    )(raw_data, row, source_blocks, t_hi, t_lo)
    near = [(i, i ^ 1) for i in range(seg_count)]
    far = [(i, i ^ 2) for i in range(seg_count)]

    def over_seg(value, pairs):
        return lax.ppermute(value, "seg", pairs)

    def slots_of(value):
        return pl.pallas_call(
            functools.partial(slot_kernel, slots, cap),
            out_shape=[send_shape, src_shape],
            in_specs=[vmem()] * 2,
            out_specs=[vmem()] * 2,
            name="slots",
        )(select, value)

    def exchange(send):
        if direct:
            return lax.all_to_all(send, "recv", split_axis=0, concat_axis=0, tiled=True)
        recv = send.reshape(windows, recv_count, cap, WIN)
        recv = lax.all_to_all(recv, "recv", split_axis=1, concat_axis=1, tiled=True)
        return recv.reshape(windows, slots, WIN)

    group = SRC_W // seg_count // cap
    low = group.bit_length() - 1
    high = recv_count.bit_length() - 1
    swap = [[(i, i ^ (1 << bit)) for i in range(recv_count)] for bit in range(low)]

    def to_all(src):
        src = double(src, seg_count, group, low, high)
        for bit in range(low - 1):
            other = lax.ppermute(src, "recv", swap[bit])
            upper = ((me >> bit) & 1) == 1
            src = jnp.concatenate(
                [jnp.where(upper, other, src), jnp.where(upper, src, other)], axis=1
            )
        return src, lax.ppermute(src, "recv", swap[low - 1])

    x2 = over_seg(x, far)
    src1 = over_seg(src, near)
    recv0 = exchange(send)
    x3 = over_seg(x2, near)
    recv1 = over_seg(recv0, near)
    send2, src2 = slots_of(x2)
    send3, src3 = slots_of(x3)
    recv2 = exchange(send2)
    recv3 = exchange(send3)
    first_two = to_all(jnp.concatenate([src, src1], axis=0))
    third, fourth = to_all(src2), to_all(src3)
    upper = ((me >> (low - 1)) & 1).reshape(1).astype(jnp.int32)
    nsrc = 2 * third[0].shape[1]
    bts, ats = [], []
    for recv, pair, start in (
        (recv0, first_two, 0), (recv1, first_two, windows), (recv2, third, 0), (recv3, fourth, 0)
    ):
        bt, at = pl.pallas_call(
            functools.partial(turn_kernel, start),
            out_shape=[
                jax.ShapeDtypeStruct((WIN // F8, windows * F8, slots), BF16),
                jax.ShapeDtypeStruct((WIN // F8, windows * F8, nsrc), BF16),
            ],
            in_specs=[smem()] + [vmem()] * 3,
            out_specs=[vmem()] * 2,
            name="turn",
        )(upper, recv, *pair)
        bts.append(bt)
        ats.append(at)

    inverse = jnp.asarray(inverse_table(WIN, seg_count * windows)[columns(WIN)].astype(BF16))
    zbs = seg_count
    per = 16
    half_steps = WIN // F8 // per
    sblk = cap
    depth = windows * F8

    def block(width):
        return pl.BlockSpec((per, depth, width), lambda i: (jnp.minimum(i, half_steps - 1), 0, 0))

    def place(i):
        at = jnp.maximum(i - half_steps, 0)
        return (at % blocks) * group + at // blocks, 0, 0

    out = pl.pallas_call(
        functools.partial(cross_kernel, zbs, sblk, per),
        out_shape=jax.ShapeDtypeStruct((nsrc, slots, WIN), BF16),
        grid=(half_steps + nsrc // sblk,),
        in_specs=[block(slots)] * zbs + [block(nsrc)] * zbs + [vmem()],
        out_specs=pl.BlockSpec((sblk, slots, WIN), place),
        scratch_shapes=[pltpu.VMEM((nsrc, WIN, slots), BF16)],
        name="cross",
    )(*bts, *ats, inverse)
    return out.reshape(blocks, nsrc // blocks, slots, WIN)


def solution(mesh):
    placed = (P("seg", "recv", None), P("recv", None), P())
    return jax.shard_map(
        steps, mesh=mesh, in_specs=placed, out_specs=P(None, "seg", "recv", None), check_vma=False
    )
```

```python
import functools
import math

import jax
import jax.numpy as jnp
import numpy as np
from jax import lax
from jax.experimental import pallas as pl
from jax.experimental.pallas import tpu as pltpu
from jax.sharding import PartitionSpec as P


WIN = 512
NB = 128
SRC_W = 128
F8 = 8
F4 = 4
F32 = jnp.float32
BF16 = jnp.bfloat16


RINGS = ()


def vmem():
    return pl.BlockSpec(memory_space=pltpu.VMEM)


def smem():
    return pl.BlockSpec(memory_space=pltpu.SMEM)


def forward_table(length):
    half = length // 2
    t = np.arange(length)[:, None]
    f = np.arange(half)[None, :]
    angles = 2.0 * math.pi * ((t * f) % length) / length
    parity = np.where(t % 2 == 0, 1.0, -1.0)
    sines = np.where(f == 0, parity, -np.sin(angles))
    return np.concatenate([np.cos(angles), sines], axis=1).astype(np.float32)


def inverse_table(length, window_total):
    half = length // 2
    lag = np.arange(length)[None, :] - half
    f = np.arange(half)[:, None]
    angles = 2.0 * math.pi * ((f * lag) % length) / length
    factor = 1.0 / (length * math.sqrt(window_total * length))
    parity = np.where(lag % 2 == 0, 1.0, -1.0)
    cosine = np.where(f == 0, factor, 2.0 * factor * np.cos(angles))
    sine = np.where(f == 0, factor * parity, -2.0 * factor * np.sin(angles))
    return np.concatenate([cosine, sine], axis=0).astype(np.float32)


def columns(length):
    return np.arange(length).reshape(2, -1, F4).transpose(1, 0, 2).reshape(-1)


def one_hots(own_row, blocks, slots, cap):
    rows = own_row.shape[1]
    own_col = jnp.broadcast_to(own_row, (rows, rows)).astype(F32).T.astype(jnp.int32)
    earlier = lax.broadcasted_iota(jnp.int32, (rows, rows), 0) < lax.broadcasted_iota(
        jnp.int32, (rows, rows), 1
    )
    hits = jnp.where((own_col == own_row) & earlier, 1.0, 0.0)
    rank = jnp.sum(hits, axis=0, keepdims=True).astype(jnp.int32)
    slot = own_row * cap + rank
    pieces = [
        jnp.where(lax.broadcasted_iota(jnp.int32, (slots, rows), 0) == slot, 1.0, 0.0)
    ]
    for block in blocks:
        place = jnp.where(own_row == block, rank, -1)
        pieces.append(
            jnp.where(lax.broadcasted_iota(jnp.int32, (cap, rows), 0) == place, 1.0, 0.0)
        )
    return jnp.concatenate(pieces, axis=0).astype(BF16)


def place_rows(x_of, windows, select, slots, send_ref, src_ref, cap):
    for k in range(windows):
        y = jnp.dot(select, x_of(k), preferred_element_type=F32).astype(BF16)
        if len(send_ref.shape) == 3:
            send_ref[k] = y[:slots]
        else:
            for d in range(slots // cap):
                send_ref[d, k] = y[d * cap : (d + 1) * cap]
        src_ref[k] = y[slots:]


def first_kernel(slots, cap, raw, row, blocks, t_hi, t_lo, x_ref, send_ref, src_ref, sel_ref):
    segs, rows, samples = raw.shape
    per = samples // WIN
    his, los = [], []
    for s in range(segs):
        for w in range(per):
            parts = []
            for b in range(WIN // NB):
                at = w * WIN + b * NB
                piece = raw[s, :, at : at + NB]
                amp = jnp.sum(jnp.abs(piece), axis=-1, keepdims=True) * (1.0 / NB) + 1e-06
                parts.append(piece / amp)
            x = jnp.concatenate(parts, axis=-1)
            hi = x.astype(BF16)
            his.append(hi)
            los.append((x - hi.astype(F32)).astype(BF16))
    hi = jnp.concatenate(his, axis=0)
    lo = jnp.concatenate(los, axis=0)
    dot = functools.partial(jnp.dot, preferred_element_type=F32)
    spec = dot(hi, t_lo[...]) + dot(lo, t_hi[...]) + dot(hi, t_hi[...])
    spec = spec.astype(BF16)
    windows = segs * per
    for k in range(windows):
        x_ref[k] = spec[k * rows : (k + 1) * rows]
    select = one_hots(row[...], [blocks[b] for b in range(blocks.shape[0])], slots, cap)
    sel_ref[...] = select
    place_rows(
        lambda k: spec[k * rows : (k + 1) * rows], windows, select, slots, send_ref, src_ref, cap
    )


def slot_kernel(slots, cap, sel_ref, x_ref, send_ref, src_ref):
    place_rows(lambda k: x_ref[k], x_ref.shape[0], sel_ref[...], slots, send_ref, src_ref, cap)


def turn_kernel(start, upper, recv, src, other, bt, at):
    windows = bt.shape[1] // F8
    wide = 256
    eye = (
        lax.broadcasted_iota(jnp.int32, (wide, wide), 0)
        == lax.broadcasted_iota(jnp.int32, (wide, wide), 1)
    ).astype(BF16)
    turn = functools.partial(
        lax.dot_general, dimension_numbers=(((1,), (1,)), ((), ())), preferred_element_type=F32
    )

    def received(k, ls):
        if len(recv.shape) == 3:
            return [recv[k, :, ls]]
        return [recv[d, k, :, ls] for d in range(recv.shape[0])]

    def sources(k, ls):
        mine, theirs = src[start + k, :, ls], other[start + k, :, ls]
        swap = upper[0] == 1
        return [jnp.where(swap, theirs, mine), jnp.where(swap, mine, theirs)]

    for load, out in ((received, bt), (sources, at)):
        n = out.shape[-1]
        for half in range(WIN // wide):
            ls = slice(half * wide, (half + 1) * wide)
            fs = slice(half * wide // F8, (half + 1) * wide // F8)
            for pair in range(windows // 2):
                both = jnp.concatenate(load(2 * pair, ls) + load(2 * pair + 1, ls), axis=0)
                y = turn(eye, both)
                y0 = y[:, :n].reshape(wide // F8, F8, n)
                y1 = y[:, n:].reshape(wide // F8, F8, n)
                out[fs, pair * 16 : (pair + 1) * 16, :] = jnp.concatenate(
                    [y0, y1], axis=1
                ).astype(BF16)


def cross_kernel(zbs, sblk, per, *refs):
    b_refs, a_refs = refs[:zbs], refs[zbs : 2 * zbs]
    inv, out, stack = refs[2 * zbs :]
    step = pl.program_id(0)
    nsrc, _, nrcv = stack.shape
    half_steps = WIN // F8 // per

    @pl.when(step < half_steps)
    def _():
        depth = zbs * b_refs[0].shape[1]
        groups = depth // F8
        iota = functools.partial(lax.broadcasted_iota, jnp.int32)
        rep = (iota((nsrc * F4, nsrc), 0) // F4 == iota((nsrc * F4, nsrc), 1)).astype(BF16)
        diag = iota((F8, depth), 1) % F4 == iota((F8, depth), 0) % F4
        place = iota((1, F8, nrcv), 1)
        low = place < F4
        turn = functools.partial(
            lax.dot_general, dimension_numbers=(((1,), (1,)), ((), ())), preferred_element_type=F32
        )
        evens, odds = [], []
        for j in range(per):
            w = jnp.concatenate([r[j] for r in b_refs], axis=0)
            v = jnp.concatenate([r[j] for r in a_refs], axis=0)
            wide = turn(rep, v).reshape(nsrc * F4 // F8, F8, depth)
            left = jnp.where(diag[None], wide, 0.0).reshape(nsrc * F4, depth).astype(BF16)
            w3 = w.astype(F32).reshape(groups, F8, nrcv)
            turned = pltpu.roll(w3, F4, 1)
            turned = jnp.where(low, turned, -turned)
            if j == 0:
                zero, nyquist = (step == 0) & (place == 0), (step == 0) & (place == F4)
                turned = jnp.where(zero, 0.0, jnp.where(nyquist, w3, turned))
                w = jnp.where(nyquist, 0.0, w3).reshape(depth, nrcv).astype(BF16)
            right = jnp.concatenate([w, turned.reshape(depth, nrcv).astype(BF16)], axis=1)
            res = jnp.dot(left, right, preferred_element_type=F32)
            real = res[:, :nrcv].reshape(nsrc // 2, F8, nrcv)
            imag = res[:, nrcv:].reshape(nsrc // 2, F8, nrcv)
            evens.append(jnp.where(low, real, pltpu.roll(imag, F4, 1)))
            odds.append(jnp.where(low, pltpu.roll(real, F4, 1), imag))
        for j in range(0, per, 2):
            at = pl.multiple_of((step * per + j) * F8, 2 * F8)
            even, odd = (jnp.concatenate(h[j : j + 2], axis=1).astype(BF16) for h in (evens, odds))
            stack[: nsrc // 2, pl.ds(at, 2 * F8), :] = even
            stack[nsrc // 2 :, pl.ds(at, 2 * F8), :] = odd

    @pl.when(step >= half_steps)
    def _():
        each = sblk // 2
        first = (step - half_steps) * each
        slab = jnp.concatenate(
            [stack[p * (nsrc // 2) + first + s] for s in range(each) for p in range(2)], axis=1
        )
        res = lax.dot_general(
            slab, inv[...], (((0,), (0,)), ((), ())), preferred_element_type=F32
        ).astype(BF16)
        for s in range(sblk):
            out[s] = res[s * nrcv : (s + 1) * nrcv]


def ring(src, seg_count):
    legs = ([], [], [])
    for z in range(seg_count):
        ways = ((z, z ^ 1, z ^ 3, z ^ 2), (z, z ^ 2, z ^ 3, z ^ 1))
        for core, way in enumerate(ways):
            for leg in range(3):
                a, b = 2 * way[leg] + core, 2 * way[leg + 1] + core
                legs[leg].append((a * seg_count + z, b * seg_count + z))
    got = [src]
    for leg in range(3):
        got.append(lax.ppermute(got[-1], ("recv", "seg"), legs[leg]))
    me = lax.axis_index("recv")
    chip = (me >> 1) ^ lax.axis_index("seg")
    one = chip == 1 + (me & 1)
    return jnp.where(chip == 0, src, jnp.where(one, got[1], jnp.where(chip == 3, got[2], got[3])))


def double(src, seg_count, group, low, high):
    me, seg = lax.axis_index("recv"), lax.axis_index("seg")
    held = [[z * group + g for g in range(group)] for z in range(seg_count)]
    for bit in range(high - 1, low - 1, -1):
        pairs = [
            (h * seg_count + z, (h ^ (1 << bit)) * seg_count + z)
            for z in range(seg_count)
            for h in held[z]
        ]
        got = lax.ppermute(src, ("recv", "seg"), pairs)
        apart = (me ^ (seg * group)) >> low
        src = jnp.where((apart & ((1 << (bit - low + 1)) - 1)) == 0, src, got)
        held = [hs + [h ^ (1 << bit) for h in hs] for hs in held]
    return src


def steps(raw_data, row_owner, source_blocks):
    recv_count = lax.axis_size("recv")
    seg_count = lax.axis_size("seg")
    segs, rows, samples = raw_data.shape
    windows = segs * samples // WIN
    cap = 2 * rows // recv_count
    slots = recv_count * cap
    blocks = source_blocks.shape[0]
    assert slots == SRC_W
    direct = cap % 16 == 0
    me = lax.axis_index("recv")
    assert seg_count == 4
    row = row_owner.reshape(1, rows)
    table = forward_table(WIN)[:, columns(WIN)]
    t_hi = table.astype(BF16)
    t_lo = (table - t_hi.astype(np.float32)).astype(BF16)
    t_hi, t_lo = jnp.asarray(t_hi), jnp.asarray(t_lo)

    send_shape = (recv_count, windows, cap, WIN) if direct else (windows, slots, WIN)
    send_shape = jax.ShapeDtypeStruct(send_shape, BF16)
    src_shape = jax.ShapeDtypeStruct((windows, blocks * cap, WIN), BF16)
    x_shape = jax.ShapeDtypeStruct((windows, rows, WIN), BF16)

    picks = slots + blocks * cap
    x, send, src, select = pl.pallas_call(
        functools.partial(first_kernel, slots, cap),
        out_shape=[x_shape, send_shape, src_shape, jax.ShapeDtypeStruct((picks, rows), BF16)],
        in_specs=[vmem(), vmem(), smem(), vmem(), vmem()],
        out_specs=[vmem()] * 4,
        name="first",
    )(raw_data, row, source_blocks, t_hi, t_lo)
    near = [(i, i ^ 1) for i in range(seg_count)]
    far = [(i, i ^ 2) for i in range(seg_count)]

    def over_seg(value, pairs):
        return lax.ppermute(value, "seg", pairs)

    def slots_of(value):
        return pl.pallas_call(
            functools.partial(slot_kernel, slots, cap),
            out_shape=[send_shape, src_shape],
            in_specs=[vmem()] * 2,
            out_specs=[vmem()] * 2,
            name="slots",
        )(select, value)

    def exchange(send):
        if direct:
            return lax.all_to_all(send, "recv", split_axis=0, concat_axis=0, tiled=True)
        recv = send.reshape(windows, recv_count, cap, WIN)
        recv = lax.all_to_all(recv, "recv", split_axis=1, concat_axis=1, tiled=True)
        return recv.reshape(windows, slots, WIN)

    group = SRC_W // seg_count // cap
    low = group.bit_length() - 1
    high = recv_count.bit_length() - 1
    swap = [[(i, i ^ (1 << bit)) for i in range(recv_count)] for bit in range(low)]

    def to_all(src, n):
        if n in RINGS and low == 1 and high == 3:
            src = ring(src, seg_count)
        else:
            src = double(src, seg_count, group, low, high)
        for bit in range(low - 1):
            other = lax.ppermute(src, "recv", swap[bit])
            upper = ((me >> bit) & 1) == 1
            src = jnp.concatenate(
                [jnp.where(upper, other, src), jnp.where(upper, src, other)], axis=1
            )
        return src, lax.ppermute(src, "recv", swap[low - 1])

    x2 = over_seg(x, far)
    src1 = over_seg(src, near)
    recv0 = exchange(send)
    x3 = over_seg(x2, near)
    recv1 = over_seg(recv0, near)
    send2, src2 = slots_of(x2)
    send3, src3 = slots_of(x3)
    recv2 = exchange(send2)
    recv3 = exchange(send3)
    first_two = to_all(jnp.concatenate([src, src1], axis=0), 0)
    third, fourth = to_all(src2, 2), to_all(src3, 3)
    upper = ((me >> (low - 1)) & 1).reshape(1).astype(jnp.int32)
    nsrc = 2 * third[0].shape[1]
    bts, ats = [], []
    for recv, pair, start in (
        (recv0, first_two, 0), (recv1, first_two, windows), (recv2, third, 0), (recv3, fourth, 0)
    ):
        bt, at = pl.pallas_call(
            functools.partial(turn_kernel, start),
            out_shape=[
                jax.ShapeDtypeStruct((WIN // F8, windows * F8, slots), BF16),
                jax.ShapeDtypeStruct((WIN // F8, windows * F8, nsrc), BF16),
            ],
            in_specs=[smem()] + [vmem()] * 3,
            out_specs=[vmem()] * 2,
            name="turn",
        )(upper, recv, *pair)
        bts.append(bt)
        ats.append(at)

    inverse = jnp.asarray(inverse_table(WIN, seg_count * windows)[columns(WIN)].astype(BF16))
    zbs = seg_count
    per = 16
    half_steps = WIN // F8 // per
    sblk = cap
    depth = windows * F8

    def block(width):
        return pl.BlockSpec((per, depth, width), lambda i: (jnp.minimum(i, half_steps - 1), 0, 0))

    def place(i):
        at = jnp.maximum(i - half_steps, 0)
        return (at % blocks) * group + at // blocks, 0, 0

    out = pl.pallas_call(
        functools.partial(cross_kernel, zbs, sblk, per),
        out_shape=jax.ShapeDtypeStruct((nsrc, slots, WIN), BF16),
        grid=(half_steps + nsrc // sblk,),
        in_specs=[block(slots)] * zbs + [block(nsrc)] * zbs + [vmem()],
        out_specs=pl.BlockSpec((sblk, slots, WIN), place),
        scratch_shapes=[pltpu.VMEM((nsrc, WIN, slots), BF16)],
        name="cross",
    )(*bts, *ats, inverse)
    return out.reshape(blocks, nsrc // blocks, slots, WIN)


def solution(mesh):
    placed = (P("seg", "recv", None), P("recv", None), P())
    return jax.shard_map(
        steps, mesh=mesh, in_specs=placed, out_specs=P(None, "seg", "recv", None), check_vma=False
    )
```

```python
import functools
import math

import jax
import jax.numpy as jnp
import numpy as np
from jax import lax
from jax.experimental import pallas as pl
from jax.experimental.pallas import tpu as pltpu
from jax.sharding import PartitionSpec as P


WIN = 512
NB = 128
SRC_W = 128
F8 = 8
F4 = 4
F32 = jnp.float32
BF16 = jnp.bfloat16


RINGS = ()


def vmem():
    return pl.BlockSpec(memory_space=pltpu.VMEM)


def smem():
    return pl.BlockSpec(memory_space=pltpu.SMEM)


def forward_table(length):
    half = length // 2
    t = np.arange(length)[:, None]
    f = np.arange(half)[None, :]
    angles = 2.0 * math.pi * ((t * f) % length) / length
    parity = np.where(t % 2 == 0, 1.0, -1.0)
    sines = np.where(f == 0, parity, -np.sin(angles))
    return np.concatenate([np.cos(angles), sines], axis=1).astype(np.float32)


def inverse_table(length, window_total):
    half = length // 2
    lag = np.arange(length)[None, :] - half
    f = np.arange(half)[:, None]
    angles = 2.0 * math.pi * ((f * lag) % length) / length
    factor = 1.0 / (length * math.sqrt(window_total * length))
    parity = np.where(lag % 2 == 0, 1.0, -1.0)
    cosine = np.where(f == 0, factor, 2.0 * factor * np.cos(angles))
    sine = np.where(f == 0, factor * parity, -2.0 * factor * np.sin(angles))
    return np.concatenate([cosine, sine], axis=0).astype(np.float32)


def columns(length):
    return np.arange(length).reshape(2, -1, F4).transpose(1, 0, 2).reshape(-1)


def one_hots(own_row, blocks, slots, cap):
    rows = own_row.shape[1]
    own_col = jnp.broadcast_to(own_row, (rows, rows)).astype(F32).T.astype(jnp.int32)
    earlier = lax.broadcasted_iota(jnp.int32, (rows, rows), 0) < lax.broadcasted_iota(
        jnp.int32, (rows, rows), 1
    )
    hits = jnp.where((own_col == own_row) & earlier, 1.0, 0.0)
    rank = jnp.sum(hits, axis=0, keepdims=True).astype(jnp.int32)
    slot = own_row * cap + rank
    pieces = [
        jnp.where(lax.broadcasted_iota(jnp.int32, (slots, rows), 0) == slot, 1.0, 0.0)
    ]
    for block in blocks:
        place = jnp.where(own_row == block, rank, -1)
        pieces.append(
            jnp.where(lax.broadcasted_iota(jnp.int32, (cap, rows), 0) == place, 1.0, 0.0)
        )
    return jnp.concatenate(pieces, axis=0).astype(BF16)


def place_rows(x_of, windows, select, slots, send_ref, src_ref, cap):
    for k in range(windows):
        y = jnp.dot(select, x_of(k), preferred_element_type=F32).astype(BF16)
        if len(send_ref.shape) == 3:
            send_ref[k] = y[:slots]
        else:
            for d in range(slots // cap):
                send_ref[d, k] = y[d * cap : (d + 1) * cap]
        src_ref[k] = y[slots:]


def first_kernel(slots, cap, raw, row, blocks, t_hi, t_lo, x_ref, sel_ref):
    segs, rows, samples = raw.shape
    per = samples // WIN
    his, los = [], []
    for s in range(segs):
        for w in range(per):
            parts = []
            for b in range(WIN // NB):
                at = w * WIN + b * NB
                piece = raw[s, :, at : at + NB]
                amp = jnp.sum(jnp.abs(piece), axis=-1, keepdims=True) * (1.0 / NB) + 1e-06
                parts.append(piece / amp)
            x = jnp.concatenate(parts, axis=-1)
            hi = x.astype(BF16)
            his.append(hi)
            los.append((x - hi.astype(F32)).astype(BF16))
    hi = jnp.concatenate(his, axis=0)
    lo = jnp.concatenate(los, axis=0)
    dot = functools.partial(jnp.dot, preferred_element_type=F32)
    spec = dot(hi, t_lo[...]) + dot(lo, t_hi[...]) + dot(hi, t_hi[...])
    spec = spec.astype(BF16)
    windows = segs * per
    for k in range(windows):
        x_ref[k] = spec[k * rows : (k + 1) * rows]
    select = one_hots(row[...], [blocks[b] for b in range(blocks.shape[0])], slots, cap)
    sel_ref[...] = select


def slot_kernel(slots, cap, sel_ref, x_ref, send_ref, src_ref):
    place_rows(lambda k: x_ref[k], x_ref.shape[0], sel_ref[...], slots, send_ref, src_ref, cap)


def turn_kernel(start, upper, recv, src, other, bt, at):
    windows = bt.shape[1] // F8
    wide = 256
    eye = (
        lax.broadcasted_iota(jnp.int32, (wide, wide), 0)
        == lax.broadcasted_iota(jnp.int32, (wide, wide), 1)
    ).astype(BF16)
    turn = functools.partial(
        lax.dot_general, dimension_numbers=(((1,), (1,)), ((), ())), preferred_element_type=F32
    )

    def received(k, ls):
        if len(recv.shape) == 3:
            return [recv[k, :, ls]]
        return [recv[d, k, :, ls] for d in range(recv.shape[0])]

    def sources(k, ls):
        mine, theirs = src[start + k, :, ls], other[start + k, :, ls]
        swap = upper[0] == 1
        return [jnp.where(swap, theirs, mine), jnp.where(swap, mine, theirs)]

    for load, out in ((received, bt), (sources, at)):
        n = out.shape[-1]
        for half in range(WIN // wide):
            ls = slice(half * wide, (half + 1) * wide)
            fs = slice(half * wide // F8, (half + 1) * wide // F8)
            for pair in range(windows // 2):
                both = jnp.concatenate(load(2 * pair, ls) + load(2 * pair + 1, ls), axis=0)
                y = turn(eye, both)
                y0 = y[:, :n].reshape(wide // F8, F8, n)
                y1 = y[:, n:].reshape(wide // F8, F8, n)
                out[fs, pair * 16 : (pair + 1) * 16, :] = jnp.concatenate(
                    [y0, y1], axis=1
                ).astype(BF16)


def cross_kernel(zbs, sblk, per, *refs):
    b_refs, a_refs = refs[:zbs], refs[zbs : 2 * zbs]
    inv, out, stack = refs[2 * zbs :]
    step = pl.program_id(0)
    nsrc, _, nrcv = stack.shape
    half_steps = WIN // F8 // per

    @pl.when(step < half_steps)
    def _():
        depth = zbs * b_refs[0].shape[1]
        groups = depth // F8
        iota = functools.partial(lax.broadcasted_iota, jnp.int32)
        rep = (iota((nsrc * F4, nsrc), 0) // F4 == iota((nsrc * F4, nsrc), 1)).astype(BF16)
        diag = iota((F8, depth), 1) % F4 == iota((F8, depth), 0) % F4
        place = iota((1, F8, nrcv), 1)
        low = place < F4
        turn = functools.partial(
            lax.dot_general, dimension_numbers=(((1,), (1,)), ((), ())), preferred_element_type=F32
        )
        evens, odds = [], []
        for j in range(per):
            w = jnp.concatenate([r[j] for r in b_refs], axis=0)
            v = jnp.concatenate([r[j] for r in a_refs], axis=0)
            wide = turn(rep, v).reshape(nsrc * F4 // F8, F8, depth)
            left = jnp.where(diag[None], wide, 0.0).reshape(nsrc * F4, depth).astype(BF16)
            w3 = w.astype(F32).reshape(groups, F8, nrcv)
            turned = pltpu.roll(w3, F4, 1)
            turned = jnp.where(low, turned, -turned)
            if j == 0:
                zero, nyquist = (step == 0) & (place == 0), (step == 0) & (place == F4)
                turned = jnp.where(zero, 0.0, jnp.where(nyquist, w3, turned))
                w = jnp.where(nyquist, 0.0, w3).reshape(depth, nrcv).astype(BF16)
            right = jnp.concatenate([w, turned.reshape(depth, nrcv).astype(BF16)], axis=1)
            res = jnp.dot(left, right, preferred_element_type=F32)
            real = res[:, :nrcv].reshape(nsrc // 2, F8, nrcv)
            imag = res[:, nrcv:].reshape(nsrc // 2, F8, nrcv)
            evens.append(jnp.where(low, real, pltpu.roll(imag, F4, 1)))
            odds.append(jnp.where(low, pltpu.roll(real, F4, 1), imag))
        for j in range(0, per, 2):
            at = pl.multiple_of((step * per + j) * F8, 2 * F8)
            even, odd = (jnp.concatenate(h[j : j + 2], axis=1).astype(BF16) for h in (evens, odds))
            stack[: nsrc // 2, pl.ds(at, 2 * F8), :] = even
            stack[nsrc // 2 :, pl.ds(at, 2 * F8), :] = odd

    @pl.when(step >= half_steps)
    def _():
        each = sblk // 2
        first = (step - half_steps) * each
        slab = jnp.concatenate(
            [stack[p * (nsrc // 2) + first + s] for s in range(each) for p in range(2)], axis=1
        )
        res = lax.dot_general(
            slab, inv[...], (((0,), (0,)), ((), ())), preferred_element_type=F32
        ).astype(BF16)
        for s in range(sblk):
            out[s] = res[s * nrcv : (s + 1) * nrcv]


def ring(src, seg_count):
    legs = ([], [], [])
    for z in range(seg_count):
        ways = ((z, z ^ 1, z ^ 3, z ^ 2), (z, z ^ 2, z ^ 3, z ^ 1))
        for core, way in enumerate(ways):
            for leg in range(3):
                a, b = 2 * way[leg] + core, 2 * way[leg + 1] + core
                legs[leg].append((a * seg_count + z, b * seg_count + z))
    got = [src]
    for leg in range(3):
        got.append(lax.ppermute(got[-1], ("recv", "seg"), legs[leg]))
    me = lax.axis_index("recv")
    chip = (me >> 1) ^ lax.axis_index("seg")
    one = chip == 1 + (me & 1)
    return jnp.where(chip == 0, src, jnp.where(one, got[1], jnp.where(chip == 3, got[2], got[3])))


def double(src, seg_count, group, low, high):
    me, seg = lax.axis_index("recv"), lax.axis_index("seg")
    held = [[z * group + g for g in range(group)] for z in range(seg_count)]
    for bit in range(high - 1, low - 1, -1):
        pairs = [
            (h * seg_count + z, (h ^ (1 << bit)) * seg_count + z)
            for z in range(seg_count)
            for h in held[z]
        ]
        got = lax.ppermute(src, ("recv", "seg"), pairs)
        apart = (me ^ (seg * group)) >> low
        src = jnp.where((apart & ((1 << (bit - low + 1)) - 1)) == 0, src, got)
        held = [hs + [h ^ (1 << bit) for h in hs] for hs in held]
    return src


def steps(raw_data, row_owner, source_blocks):
    recv_count = lax.axis_size("recv")
    seg_count = lax.axis_size("seg")
    segs, rows, samples = raw_data.shape
    windows = segs * samples // WIN
    cap = 2 * rows // recv_count
    slots = recv_count * cap
    blocks = source_blocks.shape[0]
    assert slots == SRC_W
    direct = cap % 16 == 0
    me = lax.axis_index("recv")
    assert seg_count == 4
    row = row_owner.reshape(1, rows)
    table = forward_table(WIN)[:, columns(WIN)]
    t_hi = table.astype(BF16)
    t_lo = (table - t_hi.astype(np.float32)).astype(BF16)
    t_hi, t_lo = jnp.asarray(t_hi), jnp.asarray(t_lo)

    send_shape = (recv_count, windows, cap, WIN) if direct else (windows, slots, WIN)
    send_shape = jax.ShapeDtypeStruct(send_shape, BF16)
    src_shape = jax.ShapeDtypeStruct((windows, blocks * cap, WIN), BF16)
    x_shape = jax.ShapeDtypeStruct((windows, rows, WIN), BF16)

    picks = slots + blocks * cap
    x, select = pl.pallas_call(
        functools.partial(first_kernel, slots, cap),
        out_shape=[x_shape, jax.ShapeDtypeStruct((picks, rows), BF16)],
        in_specs=[vmem(), vmem(), smem(), vmem(), vmem()],
        out_specs=[vmem()] * 2,
        name="first",
    )(raw_data, row, source_blocks, t_hi, t_lo)
    near = [(i, i ^ 1) for i in range(seg_count)]
    far = [(i, i ^ 2) for i in range(seg_count)]

    def over_seg(value, pairs):
        return lax.ppermute(value, "seg", pairs)

    def slots_of(value):
        return pl.pallas_call(
            functools.partial(slot_kernel, slots, cap),
            out_shape=[send_shape, src_shape],
            in_specs=[vmem()] * 2,
            out_specs=[vmem()] * 2,
            name="slots",
        )(select, value)

    def exchange(send):
        if direct:
            return lax.all_to_all(send, "recv", split_axis=0, concat_axis=0, tiled=True)
        recv = send.reshape(windows, recv_count, cap, WIN)
        recv = lax.all_to_all(recv, "recv", split_axis=1, concat_axis=1, tiled=True)
        return recv.reshape(windows, slots, WIN)

    group = SRC_W // seg_count // cap
    low = group.bit_length() - 1
    high = recv_count.bit_length() - 1
    swap = [[(i, i ^ (1 << bit)) for i in range(recv_count)] for bit in range(low)]

    def to_all(src, n):
        if n in RINGS and low == 1 and high == 3:
            src = ring(src, seg_count)
        else:
            src = double(src, seg_count, group, low, high)
        for bit in range(low - 1):
            other = lax.ppermute(src, "recv", swap[bit])
            upper = ((me >> bit) & 1) == 1
            src = jnp.concatenate(
                [jnp.where(upper, other, src), jnp.where(upper, src, other)], axis=1
            )
        return src, lax.ppermute(src, "recv", swap[low - 1])

    x2 = over_seg(x, far)
    send, src = slots_of(x)
    src1 = over_seg(src, near)
    recv0 = exchange(send)
    x3 = over_seg(x2, near)
    recv1 = over_seg(recv0, near)
    send2, src2 = slots_of(x2)
    send3, src3 = slots_of(x3)
    recv2 = exchange(send2)
    recv3 = exchange(send3)
    first_two = to_all(jnp.concatenate([src, src1], axis=0), 0)
    third, fourth = to_all(src2, 2), to_all(src3, 3)
    upper = ((me >> (low - 1)) & 1).reshape(1).astype(jnp.int32)
    nsrc = 2 * third[0].shape[1]
    bts, ats = [], []
    for recv, pair, start in (
        (recv0, first_two, 0), (recv1, first_two, windows), (recv2, third, 0), (recv3, fourth, 0)
    ):
        bt, at = pl.pallas_call(
            functools.partial(turn_kernel, start),
            out_shape=[
                jax.ShapeDtypeStruct((WIN // F8, windows * F8, slots), BF16),
                jax.ShapeDtypeStruct((WIN // F8, windows * F8, nsrc), BF16),
            ],
            in_specs=[smem()] + [vmem()] * 3,
            out_specs=[vmem()] * 2,
            name="turn",
        )(upper, recv, *pair)
        bts.append(bt)
        ats.append(at)

    inverse = jnp.asarray(inverse_table(WIN, seg_count * windows)[columns(WIN)].astype(BF16))
    zbs = seg_count
    per = 16
    half_steps = WIN // F8 // per
    sblk = cap
    depth = windows * F8

    def block(width):
        return pl.BlockSpec((per, depth, width), lambda i: (jnp.minimum(i, half_steps - 1), 0, 0))

    def place(i):
        at = jnp.maximum(i - half_steps, 0)
        return (at % blocks) * group + at // blocks, 0, 0

    out = pl.pallas_call(
        functools.partial(cross_kernel, zbs, sblk, per),
        out_shape=jax.ShapeDtypeStruct((nsrc, slots, WIN), BF16),
        grid=(half_steps + nsrc // sblk,),
        in_specs=[block(slots)] * zbs + [block(nsrc)] * zbs + [vmem()],
        out_specs=pl.BlockSpec((sblk, slots, WIN), place),
        scratch_shapes=[pltpu.VMEM((nsrc, WIN, slots), BF16)],
        name="cross",
    )(*bts, *ats, inverse)
    return out.reshape(blocks, nsrc // blocks, slots, WIN)


def solution(mesh):
    placed = (P("seg", "recv", None), P("recv", None), P())
    return jax.shard_map(
        steps, mesh=mesh, in_specs=placed, out_specs=P(None, "seg", "recv", None), check_vma=False
    )
```
